32 devices in a mesh: replica: 8 (over y, x, core), tensor: 4 (over z).
Axes of the slice: x: 2, y: 2, z: 4, core: 2. Of those that a mesh axis runs over, the one named last changes fastest.
Arguments:
- queries: bfloat16 [8, 512, 2560], P('replica', None, 'tensor'), may hold values from -160 to 160
- key_rows: bfloat16 [8, 512, 2560], P('replica', None, 'tensor'), may hold values from -4 to 4
- value_rows: bfloat16 [8, 512, 2560], P('replica', None, 'tensor'), may hold values from -6 to 6
- out_grads: bfloat16 [8, 512, 1024], P('replica', 'tensor'), may hold values from -6 to 6
- inner_weights: bfloat16 [8, 20, 128, 1024], P('replica', 'tensor'), may hold values from -0.15625 to 0.15625
- adam_first: bfloat16 [8, 20, 128, 1024], P('replica', 'tensor'), may hold values from -12 to 12
- adam_second: bfloat16 [8, 20, 128, 1024], P('replica', 'tensor'), may hold values from 1 to 16
- anchor: bfloat16 [20, 128, 1024], P('tensor'), may hold values from -0.125 to 0.125
- momentum: float32 [20, 128, 1024], P('tensor', 'replica'), may hold values from -0.06 to 0.06
Outputs:
- query_grads: bfloat16 [8, 512, 2560], P('replica', None, 'tensor')
- key_grads: bfloat16 [8, 512, 2560], P('replica', None, 'tensor')
- value_grads: bfloat16 [8, 512, 2560], P('replica', None, 'tensor')
- new_first: bfloat16 [8, 20, 128, 1024], P('replica', 'tensor')
- new_second: bfloat16 [8, 20, 128, 1024], P('replica', 'tensor')
- new_anchor: bfloat16 [20, 128, 1024], P('tensor')
- new_momentum: float32 [20, 128, 1024], P('tensor', 'replica')
The draws below stay inside these ranges and needn't reach their ends.
All inputs are finite; a program needn't handle non-finite values.
Results may differ from the reference program's by a relative error of at most 0.028.
Values may be sent and summed in bfloat16 or wider, within the bound.
A program may use at most 64 MiB of HBM per device.

```python
import math
import jax
import jax.numpy as jnp
from jax import lax

D = 1024
DH = 128
LEN = 512
WORKERS = 8
HEADS = 20
INNER = 2560


def drawn_pair(key):
    base = jax.random.fold_in(key, 11)
    query_key, row_key = jax.random.split(base, 2)
    shape = (WORKERS, HEADS, LEN, DH)
    query_heads = jnp.clip(jax.random.normal(query_key, shape, jnp.float32), -6.0, 6.0)
    key_heads = jnp.clip(jax.random.normal(row_key, shape, jnp.float32), -4.0, 4.0)
    return (query_heads, key_heads)


def widened(head_array):
    return jnp.transpose(head_array, (0, 2, 1, 3)).reshape(WORKERS, LEN, HEADS * DH).astype(jnp.bfloat16)


def draw_queries(key, part):
    return widened(drawn_pair(key)[0])


def draw_key_rows(key, part):
    return widened(drawn_pair(key)[1])


def strengthened(entries, stream_key, source, target, blocks, factor):
    def block_of(dim):
        return (jnp.arange(entries.shape[dim]) // (entries.shape[dim] // blocks)).reshape((-1,) + (1,) * (entries.ndim - 1 - dim))

    first = jax.random.permutation(stream_key, blocks)[block_of(target)]
    second = (block_of(target) + blocks // 2) % blocks
    return jnp.where((block_of(source) == first) | (block_of(source) == second), factor * entries, entries)


def levels(own_key, dims, shards, smallest, top_value):
    def one(axis_at, blocks):
        steps = jax.random.uniform(jax.random.fold_in(jax.random.fold_in(own_key, 6), axis_at), (blocks,), jnp.float32, smallest / len(shards), top_value / len(shards))
        return jnp.repeat(jnp.exp(steps), dims[axis_at] // blocks).reshape((-1,) + (1,) * (len(dims) - axis_at - 1))

    factor_of = one(*shards[0])
    for cut in shards[1:]:
        factor_of = factor_of * one(*cut)
    return factor_of


def gaussian(key, shape, scale, reach, cuts=(), held_as=jnp.bfloat16):
    drawn = jax.random.normal(key, shape, jnp.float32) * scale
    if len(cuts) > 0:
        drawn = levels(key, shape, cuts, -0.22, 0.18) * drawn
    return jnp.clip(drawn, min=-reach, max=reach).astype(held_as)


def bell_draw_with(rng, extent, deviation, limit, cuts, heavy, held_as=jnp.bfloat16):
    values = deviation * jax.random.normal(rng, extent, jnp.float32)
    if cuts:
        values = values * levels(rng, extent, cuts, -0.22, 0.18)
    return jnp.clip(strengthened(values, jax.random.fold_in(rng, 3), *heavy), -limit, limit).astype(held_as)


def setup_inputs(seed: int = 0) -> dict:
    key_list = jax.random.split(jax.random.key(seed), 10)
    queries = draw_queries(jax.random.fold_in(key_list[9], 71), 0)
    key_rows = draw_key_rows(jax.random.fold_in(key_list[9], 71), 0)
    value_rows = gaussian(key_list[2], (WORKERS, LEN, INNER), 1.0, 6.0, ((0, 8), (2, 4)))
    out_grads = gaussian(key_list[3], (WORKERS, LEN, D), 1.0, 6.0, ((0, 8), (1, 4)))
    inner_weights = bell_draw_with(key_list[4], (WORKERS, HEADS, DH, D), INNER ** -0.5, 0.15625, ((0, 8), (1, 4)), (0, 2, 8, 2.0))
    adam_first = gaussian(key_list[5], (WORKERS, HEADS, DH, D), 2.0, 12.0, ((0, 8), (1, 4)))
    adam_second = jnp.clip(jnp.exp(math.log(16.0) - 2.7725887 * jax.random.uniform(key_list[6], (WORKERS, HEADS, DH, D), jnp.float32) ** levels(key_list[6], (WORKERS, HEADS, DH, D), ((0, 8), (1, 4)), -0.2, 0.2)), 1.0, 16.0).astype(jnp.bfloat16)
    anchor = gaussian(key_list[7], (HEADS, DH, D), INNER ** -0.5, 0.125, ((0, 4),))
    momentum = gaussian(key_list[8], (HEADS, DH, D), 0.01, 0.06, ((0, 4), (1, 8)), jnp.float32)
    return dict(queries=queries, key_rows=key_rows, value_rows=value_rows, out_grads=out_grads, inner_weights=inner_weights, adam_first=adam_first, adam_second=adam_second, anchor=anchor, momentum=momentum)


beta_first = 0.9
beta_second = 0.95
correct_first = 0.9999734386011124
correct_second = 0.994079470779666
inner_rate = 0.01
decay_rate = 0.1
epsilon = 1e-08
outer_rate = 0.7
outer_beta = 0.9
highest = lax.Precision.HIGHEST

def lowered(values):
    return lax.optimization_barrier(values.astype(jnp.bfloat16)).astype(jnp.float32)

def worker_step(queries, key_rows, value_rows, out_grads, inner_weights, adam_first, adam_second, anchor_wide):
    score_scale = 1.0 / math.sqrt(DH)
    query_heads = queries.astype(jnp.float32).reshape(LEN, HEADS, DH)
    key_heads = key_rows.astype(jnp.float32).reshape(LEN, HEADS, DH)
    value_heads = value_rows.astype(jnp.float32).reshape(LEN, HEADS, DH)
    grads_out = out_grads.astype(jnp.float32)
    previous = inner_weights.astype(jnp.float32)
    scores = jnp.einsum('qhc,khc->hqk', query_heads, key_heads, precision=highest) * score_scale
    probs = jax.nn.softmax(scores, axis=-1)
    probs_low = lowered(probs)
    attention = lowered(jnp.einsum('hqk,khc->qhc', probs_low, value_heads, precision=highest))
    grad_proj = jnp.einsum('qhc,qd->hcd', attention, grads_out, precision=highest)
    grad_attn = lowered(jnp.einsum('qd,hcd->qhc', grads_out, previous, precision=highest))
    value_grads = jnp.einsum('hqk,qhc->khc', probs_low, grad_attn, precision=highest).astype(jnp.bfloat16)
    grad_probs = jnp.einsum('qhc,khc->hqk', grad_attn, value_heads, precision=highest)
    row_dot = jnp.einsum('qhc,qhc->hq', grad_attn, attention, precision=highest)
    grad_scores = lowered(probs * (grad_probs - row_dot[:, :, None]))
    query_grads = (jnp.einsum('hqk,khc->qhc', grad_scores, key_heads, precision=highest) * score_scale).astype(jnp.bfloat16)
    key_grads = (jnp.einsum('hqk,qhc->khc', grad_scores, query_heads, precision=highest) * score_scale).astype(jnp.bfloat16)
    first_moment = beta_first * adam_first.astype(jnp.float32) + (1.0 - beta_first) * grad_proj
    second_moment = beta_second * adam_second.astype(jnp.float32) + (1.0 - beta_second) * grad_proj * grad_proj
    stepped = previous - inner_rate * (first_moment / correct_first / (jnp.sqrt(second_moment / correct_second) + epsilon) + decay_rate * previous)
    delta_terms = (anchor_wide - stepped).astype(jnp.bfloat16)
    return (query_grads.reshape(LEN, INNER), key_grads.reshape(LEN, INNER), value_grads.reshape(LEN, INNER), first_moment.astype(jnp.bfloat16), second_moment.astype(jnp.bfloat16), delta_terms)

def reference(queries, key_rows, value_rows, out_grads, inner_weights, adam_first, adam_second, anchor, momentum):
    anchor_wide = anchor.astype(jnp.float32)

    def visit(summed, inputs):
        results = worker_step(*inputs, anchor_wide)
        deltas = lax.optimization_barrier(results[5]).astype(jnp.float32)
        return (summed + deltas, results[:5])
    summed, stacked = lax.scan(visit, jnp.zeros((HEADS, DH, D), jnp.float32), (queries, key_rows, value_rows, out_grads, inner_weights, adam_first, adam_second))
    average = summed / WORKERS
    new_momentum = outer_beta * momentum + average
    new_anchor = (anchor_wide - outer_rate * (average + outer_beta * new_momentum)).astype(jnp.bfloat16)
    return (stacked[0], stacked[1], stacked[2], stacked[3], stacked[4], new_anchor, new_momentum)
```

```python
import functools
import math

import jax
import jax.numpy as jnp
from jax import lax
from jax.experimental import pallas as pl
from jax.experimental.pallas import tpu as pltpu
from jax.sharding import PartitionSpec as P

DH = 128
CHUNKS = 4
MESH = pl.DeviceIdType.MESH

beta_first = 0.9
beta_second = 0.95
correct_first = 0.9999734386011124
correct_second = 0.994079470779666
inner_rate = 0.01
decay_rate = 0.1
epsilon = 1e-08
outer_rate = 0.7
outer_beta = 0.9

F32 = jnp.float32
BF16 = jnp.bfloat16


def dot(a, b, ca, cb):
    return lax.dot_general(a, b, (((ca,), (cb,)), ((), ())), preferred_element_type=F32)


def kernel(
    tensors,
    workers,
    q_hbm, k_hbm, v_hbm, g_hbm, w_hbm, m1_hbm, m2_hbm, anchor_hbm, mom_hbm,
    dq_hbm, dk_hbm, dv_hbm, n1_hbm, n2_hbm, na_hbm, nm_hbm,
    q, k, v, g, w, m1, m2, anchor, mom,
    dq, dk, dv, n1, n2, na, nm,
    probs, att, att_t, ds, delta, from_partner, pair, from_peers,
    in_sem, out_sem,
    g_send, g_recv, p_send, p_recv, r_send, r_recv, a_send, a_recv, f_send, f_recv,
):
    heads = w.shape[0]
    width = g.shape[2]
    length = q.shape[0]
    rows = g.shape[1]
    slab = mom.shape[1]
    chips = workers // 2
    cw = width // CHUNKS
    scale = 1.0 / math.sqrt(DH)

    i = lax.axis_index("tensor")
    r = lax.axis_index("replica")
    chip = r // 2
    core = r % 2
    partner = chip * 2 + 1 - core
    has_left = i > 0
    has_right = i < tensors - 1

    def peer(step):
        return lax.rem(chip + step, chips) * 2 + core

    def source(step):
        return lax.rem(chip + chips - step, chips)

    barrier = pltpu.get_barrier_semaphore()

    @pl.when(has_left)
    def _():
        pl.semaphore_signal(barrier, inc=1, device_id={"tensor": i - 1}, device_id_type=MESH)

    @pl.when(has_right)
    def _():
        pl.semaphore_signal(barrier, inc=1, device_id={"tensor": i + 1}, device_id_type=MESH)

    pl.semaphore_signal(barrier, inc=1, device_id={"replica": partner}, device_id_type=MESH)
    for step in range(1, chips):
        pl.semaphore_signal(barrier, inc=1, device_id={"replica": peer(step)}, device_id_type=MESH)

    loads = [
        pltpu.make_async_copy(s, d, in_sem.at[n])
        for n, (s, d) in enumerate(
            [
                (q_hbm, q), (k_hbm, k), (v_hbm, v), (g_hbm, g.at[i]), (w_hbm, w),
                (m1_hbm, m1), (m2_hbm, m2), (anchor_hbm, anchor), (mom_hbm, mom),
            ]
        )
    ]
    for load in loads:
        load.start()

    inner = jnp.logical_and(has_left, has_right)

    @pl.when(inner)
    def _():
        pl.semaphore_wait(barrier, chips + 2)

    @pl.when(jnp.logical_not(inner))
    def _():
        pl.semaphore_wait(barrier, chips + 1)

    def cols(c):
        return pl.ds(c * cw, cw)

    def right_copy(block, s, c, own=False):
        src = g_hbm.at[:, cols(c)] if own else g.at[block, :, cols(c)]
        return pltpu.make_async_remote_copy(
            src_ref=src, dst_ref=g.at[block, :, cols(c)],
            send_sem=g_send.at[0, s, c], recv_sem=g_recv.at[0, s, c],
            device_id={"tensor": i + 1}, device_id_type=MESH,
        )

    def left_copy(block, s, c, own=False):
        src = g_hbm.at[:, cols(c)] if own else g.at[block, :, cols(c)]
        return pltpu.make_async_remote_copy(
            src_ref=src, dst_ref=g.at[block, :, cols(c)],
            send_sem=g_send.at[1, s, c], recv_sem=g_recv.at[1, s, c],
            device_id={"tensor": i - 1}, device_id_type=MESH,
        )

    def own_send(c):
        @pl.when(has_right)
        def _():
            right_copy(i, 0, c, True).start()

        @pl.when(has_left)
        def _():
            left_copy(i, 0, c, True).start()

    def relay(c, s):
        @pl.when(i - 1 - s >= 0)
        def _():
            block = i - 1 - s
            right_copy(block, s, c).wait_recv()
            if s + 1 <= tensors - 2:
                @pl.when(has_right)
                def _():
                    right_copy(block, s + 1, c).start()

        @pl.when(i + 1 + s < tensors)
        def _():
            block = i + 1 + s
            left_copy(block, s, c).wait_recv()
            if s + 1 <= tensors - 2:
                @pl.when(has_left)
                def _():
                    left_copy(block, s + 1, c).start()

    def drain_gather():
        for c in range(CHUNKS):
            for s in range(tensors - 1):
                @pl.when(jnp.logical_and(has_right, i - s >= 0))
                def _():
                    right_copy(i - s, s, c, s == 0).wait_send()

                @pl.when(jnp.logical_and(has_left, i + s < tensors))
                def _():
                    left_copy(i + s, s, c, s == 0).wait_send()

    tile = 128

    def forward(h):
        hc = pl.ds(h * DH, DH)
        kh = k[:, hc]
        vh = v[:, hc]
        for t in range(length // tile):
            tr = pl.ds(t * tile, tile)
            s = dot(q[tr, hc], kh, 1, 1) * scale
            e = jnp.exp(s - jnp.max(s, axis=-1, keepdims=True))
            p = (e / jnp.sum(e, axis=-1, keepdims=True)).astype(BF16)
            probs[h, tr, :] = p
            a = dot(p, vh, 1, 0)
            att[tr, hc] = a.astype(BF16)
            att_t[h, :, tr] = a.T.astype(BF16)

    def adam(c):
        def body(h, carry):
            gb = g[:, :, cols(c)].reshape(length, cw)
            grad = dot(att_t[h], gb, 1, 0)
            first = beta_first * m1[h, :, cols(c)].astype(F32) + (1.0 - beta_first) * grad
            second = (
                beta_second * m2[h, :, cols(c)].astype(F32) + (1.0 - beta_second) * grad * grad
            )
            n1[h, :, cols(c)] = first.astype(BF16)
            n2[h, :, cols(c)] = second.astype(BF16)
            old = w[h, :, cols(c)].astype(F32)
            stepped = old - inner_rate * (
                first / correct_first / (jnp.sqrt(second / correct_second) + epsilon)
                + decay_rate * old
            )
            an = anchor[h, :, :, cols(c)].astype(F32)
            d = an - stepped.reshape(workers, slab, cw)
            for x in range(workers):
                delta[c, x % 2, x // 2, h] = d[x].astype(BF16)
            return carry

        lax.fori_loop(0, heads, body, 0)

    def partner_copy(c):
        return pltpu.make_async_remote_copy(
            src_ref=delta.at[c, 1 - core], dst_ref=from_partner.at[c],
            send_sem=p_send.at[c], recv_sem=p_recv.at[c],
            device_id={"replica": partner}, device_id_type=MESH,
        )

    def peer_copy(c, step):
        return pltpu.make_async_remote_copy(
            src_ref=pair.at[c, lax.rem(chip + step, chips)], dst_ref=from_peers.at[c, step - 1],
            send_sem=r_send.at[c, step - 1], recv_sem=r_recv.at[c, step - 1],
            device_id={"replica": peer(step)}, device_id_type=MESH,
        )

    def pair_sum(c):
        partner_copy(c).wait_recv()
        for x in range(chips):
            pair[c, x] = (
                delta[c, core, x].astype(F32) + from_partner[c, x].astype(F32)
            ).astype(BF16)
        for step in range(1, chips):
            peer_copy(c, step).start()

    def spread(c, block, step):
        return pltpu.make_async_remote_copy(
            src_ref=na.at[:, block, :, cols(c)], dst_ref=na.at[:, block, :, cols(c)],
            send_sem=a_send.at[c, step - 1], recv_sem=a_recv.at[c, step - 1],
            device_id={"replica": peer(step)}, device_id_type=MESH,
        )

    def across(c, block, step):
        return pltpu.make_async_remote_copy(
            src_ref=na.at[:, block, :, cols(c)], dst_ref=na.at[:, block, :, cols(c)],
            send_sem=f_send.at[c, step], recv_sem=f_recv.at[c, step],
            device_id={"replica": partner}, device_id_type=MESH,
        )

    def outer(c):
        total = delta[c, core, chip].astype(F32) + from_partner[c, chip].astype(F32)
        for step in range(1, chips):
            peer_copy(c, step).wait_recv()
            total = total + from_peers[c, step - 1].astype(F32)
        average = total / workers
        moved = outer_beta * mom[:, :, cols(c)] + average
        nm[:, :, cols(c)] = moved
        part = anchor[:, r, :, cols(c)].astype(F32)
        na[:, r, :, cols(c)] = (
            part - outer_rate * (average + outer_beta * moved)
        ).astype(BF16)
        for step in range(1, chips):
            spread(c, r, step).start()
        across(c, r, 0).start()

    def pass_on(c):
        for step in range(1, chips):
            block = source(step) * 2 + core
            spread(c, block, step).wait_recv()
            across(c, block, step).start()

    def anchor_out(c):
        return pltpu.make_async_copy(
            na.at[:, :, :, cols(c)], na_hbm.at[:, :, :, cols(c)], out_sem.at[5 + c]
        )

    def finish(c):
        for step in range(chips):
            across(c, source(step) * 2 + 1 - core, step).wait_recv()
        anchor_out(c).start()

    def backward(h):
        hc = pl.ds(h * DH, DH)
        kh = k[:, hc]
        vh = v[:, hc]
        ga = dot(g[...].reshape(length, width), w[h], 1, 1).astype(BF16)
        for t in range(length // tile):
            tr = pl.ds(t * tile, tile)
            gt = ga[t * tile:(t + 1) * tile]
            row = jnp.sum(gt.astype(F32) * att[tr, hc].astype(F32), axis=-1, keepdims=True)
            gp = dot(gt, vh, 1, 1)
            s = (probs[h, tr, :].astype(F32) * (gp - row)).astype(BF16)
            ds[tr, :] = s
            dq[tr, hc] = (dot(s, kh, 1, 0) * scale).astype(BF16)
        dv[:, hc] = dot(ga, probs[h], 0, 0).T.astype(BF16)
        dk[:, hc] = (dot(q[:, hc], ds[...], 0, 0) * scale).T.astype(BF16)

    own_send(0)
    own_send(1)
    loads[0].wait()
    loads[1].wait()
    loads[2].wait()
    for h in range(heads):
        forward(h)
        if h < tensors - 1:
            relay(0, h)
    for s in range(heads, tensors - 1):
        relay(0, s)
    for load in loads[3:]:
        load.wait()
    for c in range(CHUNKS):
        if c > 0:
            for s in range(tensors - 1):
                relay(c, s)
        if c + 2 < CHUNKS:
            own_send(c + 2)
        adam(c)
        partner_copy(c).start()
        if c > 0:
            outer(c - 1)
        pair_sum(c)
        if c > 0:
            pass_on(c - 1)
    last = CHUNKS - 1
    stores = [
        pltpu.make_async_copy(s, d, out_sem.at[n])
        for n, (s, d) in enumerate([(dq, dq_hbm), (dk, dk_hbm), (dv, dv_hbm), (n1, n1_hbm), (n2, n2_hbm)])
    ]
    stores[3].start()
    stores[4].start()
    backward(0)
    backward(1)
    outer(last)
    backward(2)
    backward(3)
    pass_on(last)
    for h in range(4, heads):
        backward(h)
    store_mom = pltpu.make_async_copy(nm, nm_hbm, out_sem.at[5 + CHUNKS])
    store_mom.start()
    for store in stores[:3]:
        store.start()
    for c in range(CHUNKS):
        finish(c)
    drain_gather()
    for c in range(CHUNKS):
        partner_copy(c).wait_send()
        for step in range(1, chips):
            peer_copy(c, step).wait_send()
            spread(c, r, step).wait_send()
        for step in range(chips):
            across(c, source(step) * 2 + core, step).wait_send()
        anchor_out(c).wait()
    for store in stores:
        store.wait()
    store_mom.wait()


def local(tensors, workers, queries, key_rows, value_rows, out_grads, inner_weights, adam_first,
          adam_second, anchor, momentum):
    length, inner = queries.shape[1:]
    rows, width = out_grads.shape[1:]
    heads = inner_weights.shape[1]
    slab = momentum.shape[1]
    chips = workers // 2
    cw = width // CHUNKS
    qs = (length, inner)
    ws = (heads, DH, width)
    an = (heads, workers, slab, width)
    ms = (heads, slab, width)
    S = jax.ShapeDtypeStruct
    hbm = pl.BlockSpec(memory_space=pltpu.HBM)
    V = pltpu.VMEM
    D = pltpu.SemaphoreType.DMA
    outs = pl.pallas_call(
        functools.partial(kernel, tensors, workers),
        out_shape=[
            S(qs, BF16), S(qs, BF16), S(qs, BF16), S(ws, BF16), S(ws, BF16), S(an, BF16), S(ms, F32)
        ],
        in_specs=[hbm] * 9,
        out_specs=[hbm] * 7,
        scratch_shapes=[
            V(qs, BF16), V(qs, BF16), V(qs, BF16), V((tensors, rows, width), BF16),
            V(ws, BF16), V(ws, BF16), V(ws, BF16), V(an, BF16), V(ms, F32),
            V(qs, BF16), V(qs, BF16), V(qs, BF16), V(ws, BF16), V(ws, BF16), V(an, BF16), V(ms, F32),
            V((heads, length, length), BF16), V(qs, BF16), V((heads, DH, length), BF16),
            V((length, length), BF16),
            V((CHUNKS, 2, chips, heads, slab, cw), BF16),
            V((CHUNKS, chips, heads, slab, cw), BF16),
            V((CHUNKS, chips, heads, slab, cw), BF16),
            V((CHUNKS, chips - 1, heads, slab, cw), BF16),
            D((9,)), D((6 + CHUNKS,)),
            D((2, tensors - 1, CHUNKS)), D((2, tensors - 1, CHUNKS)),
            D((CHUNKS,)), D((CHUNKS,)),
            D((CHUNKS, chips - 1)), D((CHUNKS, chips - 1)),
            D((CHUNKS, chips - 1)), D((CHUNKS, chips - 1)),
            D((CHUNKS, chips)), D((CHUNKS, chips)),
        ],
        compiler_params=pltpu.CompilerParams(collective_id=0, has_side_effects=True),
        name="sync",
    )(
        queries[0], key_rows[0], value_rows[0], out_grads[0], inner_weights[0], adam_first[0],
        adam_second[0], anchor.reshape(an), momentum,
    )
    dq, dk, dv, n1, n2, na, nm = outs
    return dq[None], dk[None], dv[None], n1[None], n2[None], na.reshape(anchor.shape), nm


def solution(mesh):
    workers = P("replica", "tensor", None, None)
    heads = P("replica", None, "tensor")
    specs = (
        heads, heads, heads, P("replica", "tensor", None), workers, workers, workers,
        P("tensor", None, None), P("tensor", "replica", None),
    )
    outs = (
        heads, heads, heads, workers, workers, P("tensor", None, None), P("tensor", "replica", None)
    )
    body = functools.partial(local, mesh.shape["tensor"], mesh.shape["replica"])
    return jax.shard_map(body, mesh=mesh, in_specs=specs, out_specs=outs, check_vma=False)
```

```python
import functools
import math

import jax
import jax.numpy as jnp
from jax import lax
from jax.experimental import pallas as pl
from jax.experimental.pallas import tpu as pltpu
from jax.sharding import PartitionSpec as P

DH = 128
CHUNKS = 2
TILE = 512
VMEM_BYTES = 67043328
SPARE = 2**17
MESH = pl.DeviceIdType.MESH

beta_first = 0.9
beta_second = 0.95
correct_first = 0.9999734386011124
correct_second = 0.994079470779666
inner_rate = 0.01
decay_rate = 0.1
epsilon = 1e-08
outer_rate = 0.7
outer_beta = 0.9

F32 = jnp.float32
BF16 = jnp.bfloat16


def dot(a, b, ca, cb):
    return lax.dot_general(a, b, (((ca,), (cb,)), ((), ())), preferred_element_type=F32)


def kernel(
    tensors,
    workers,
    q_hbm, k_hbm, v_hbm, g_hbm, w_hbm, m1_hbm, m2_hbm, anchor_hbm, mom_hbm,
    dq, dk, dv, n1, n2, na, nm,
    q, k, v, g, w, m1, m2, anchor, mom,
    probs, att, att_t, ds, delta, from_partner, pair, from_peers,
    in_sem,
    g_send, g_recv, p_send, p_recv, r_send, r_recv, a_send, a_recv, f_send, f_recv,
):
    heads = w.shape[0]
    width = g.shape[2]
    length = q.shape[0]
    rows = g.shape[1]
    slab = mom.shape[1]
    chips = workers // 2
    cw = width // CHUNKS
    scale = 1.0 / math.sqrt(DH)

    i = lax.axis_index("tensor")
    r = lax.axis_index("replica")
    chip = r // 2
    core = r % 2
    partner = chip * 2 + 1 - core
    has_left = i > 0
    has_right = i < tensors - 1

    def peer(step):
        return lax.rem(chip + step, chips) * 2 + core

    def source(step):
        return lax.rem(chip + chips - step, chips)

    barrier = pltpu.get_barrier_semaphore()

    @pl.when(has_left)
    def _():
        pl.semaphore_signal(barrier, inc=1, device_id={"tensor": i - 1}, device_id_type=MESH)

    @pl.when(has_right)
    def _():
        pl.semaphore_signal(barrier, inc=1, device_id={"tensor": i + 1}, device_id_type=MESH)

    pl.semaphore_signal(barrier, inc=1, device_id={"replica": partner}, device_id_type=MESH)
    for step in range(1, chips):
        pl.semaphore_signal(barrier, inc=1, device_id={"replica": peer(step)}, device_id_type=MESH)

    loads = [
        pltpu.make_async_copy(s, d, in_sem.at[n])
        for n, (s, d) in enumerate(
            [
                (q_hbm, q), (k_hbm, k), (v_hbm, v), (g_hbm, g.at[i]), (w_hbm, w),
                (m1_hbm, m1), (m2_hbm, m2), (anchor_hbm, anchor), (mom_hbm, mom),
            ]
        )
    ]
    for load in loads:
        load.start()

    inner = jnp.logical_and(has_left, has_right)

    @pl.when(inner)
    def _():
        pl.semaphore_wait(barrier, chips + 2)

    @pl.when(jnp.logical_not(inner))
    def _():
        pl.semaphore_wait(barrier, chips + 1)

    def cols(c):
        return pl.ds(c * cw, cw)

    def right_copy(block, s, c, own=False):
        src = g_hbm.at[:, cols(c)] if own else g.at[block, :, cols(c)]
        return pltpu.make_async_remote_copy(
            src_ref=src, dst_ref=g.at[block, :, cols(c)],
            send_sem=g_send.at[0, s, c], recv_sem=g_recv.at[0, s, c],
            device_id={"tensor": i + 1}, device_id_type=MESH,
        )

    def left_copy(block, s, c, own=False):
        src = g_hbm.at[:, cols(c)] if own else g.at[block, :, cols(c)]
        return pltpu.make_async_remote_copy(
            src_ref=src, dst_ref=g.at[block, :, cols(c)],
            send_sem=g_send.at[1, s, c], recv_sem=g_recv.at[1, s, c],
            device_id={"tensor": i - 1}, device_id_type=MESH,
        )

    def own_send(c):
        @pl.when(has_right)
        def _():
            right_copy(i, 0, c, True).start()

        @pl.when(has_left)
        def _():
            left_copy(i, 0, c, True).start()

    def relay(c, s):
        @pl.when(i - 1 - s >= 0)
        def _():
            block = i - 1 - s
            right_copy(block, s, c).wait_recv()
            if s + 1 <= tensors - 2:
                @pl.when(has_right)
                def _():
                    right_copy(block, s + 1, c).start()

        @pl.when(i + 1 + s < tensors)
        def _():
            block = i + 1 + s
            left_copy(block, s, c).wait_recv()
            if s + 1 <= tensors - 2:
                @pl.when(has_left)
                def _():
                    left_copy(block, s + 1, c).start()

    def drain_gather():
        for c in range(CHUNKS):
            for s in range(tensors - 1):
                @pl.when(jnp.logical_and(has_right, i - s >= 0))
                def _():
                    right_copy(i - s, s, c, s == 0).wait_send()

                @pl.when(jnp.logical_and(has_left, i + s < tensors))
                def _():
                    left_copy(i + s, s, c, s == 0).wait_send()

    tile = TILE

    def forward(h):
        hc = pl.ds(h * DH, DH)
        kh = k[:, hc]
        vh = v[:, hc]
        for t in range(length // tile):
            tr = pl.ds(t * tile, tile)
            s = dot(q[tr, hc], kh, 1, 1) * scale
            e = jnp.exp(s - jnp.max(s, axis=-1, keepdims=True))
            p = (e / jnp.sum(e, axis=-1, keepdims=True)).astype(BF16)
            probs[h, tr, :] = p
            a = dot(p, vh, 1, 0)
            att[tr, hc] = a.astype(BF16)
            att_t[h, :, tr] = a.T.astype(BF16)

    def adam(c):
        def body(h, carry):
            gb = g[:, :, cols(c)].reshape(length, cw)
            grad = dot(att_t[h], gb, 1, 0)
            first = beta_first * m1[h, :, cols(c)].astype(F32) + (1.0 - beta_first) * grad
            second = (
                beta_second * m2[h, :, cols(c)].astype(F32) + (1.0 - beta_second) * grad * grad
            )
            n1[h, :, cols(c)] = first.astype(BF16)
            n2[h, :, cols(c)] = second.astype(BF16)
            old = w[h, :, cols(c)].astype(F32)
            stepped = old - inner_rate * (
                first / correct_first / (jnp.sqrt(second / correct_second) + epsilon)
                + decay_rate * old
            )
            an = anchor[h, :, :, cols(c)].astype(F32)
            d = an - stepped.reshape(workers, slab, cw)
            for x in range(workers):
                delta[c, x % 2, x // 2, h] = d[x].astype(BF16)
            return carry

        lax.fori_loop(0, heads, body, 0)

    def partner_copy(c):
        return pltpu.make_async_remote_copy(
            src_ref=delta.at[c, 1 - core], dst_ref=from_partner.at[c],
            send_sem=p_send.at[c], recv_sem=p_recv.at[c],
            device_id={"replica": partner}, device_id_type=MESH,
        )

    def peer_copy(c, step):
        return pltpu.make_async_remote_copy(
            src_ref=pair.at[c, lax.rem(chip + step, chips)], dst_ref=from_peers.at[c, step - 1],
            send_sem=r_send.at[c, step - 1], recv_sem=r_recv.at[c, step - 1],
            device_id={"replica": peer(step)}, device_id_type=MESH,
        )

    def pair_sum(c):
        partner_copy(c).wait_recv()
        for x in range(chips):
            pair[c, x] = (
                delta[c, core, x].astype(F32) + from_partner[c, x].astype(F32)
            ).astype(BF16)
        for step in range(1, chips):
            peer_copy(c, step).start()

    def spread(c, block, step):
        return pltpu.make_async_remote_copy(
            src_ref=na.at[:, block, :, cols(c)], dst_ref=na.at[:, block, :, cols(c)],
            send_sem=a_send.at[c, step - 1], recv_sem=a_recv.at[c, step - 1],
            device_id={"replica": peer(step)}, device_id_type=MESH,
        )

    def across(c, block, step):
        return pltpu.make_async_remote_copy(
            src_ref=na.at[:, block, :, cols(c)], dst_ref=na.at[:, block, :, cols(c)],
            send_sem=f_send.at[c, step], recv_sem=f_recv.at[c, step],
            device_id={"replica": partner}, device_id_type=MESH,
        )

    def outer(c):
        total = delta[c, core, chip].astype(F32) + from_partner[c, chip].astype(F32)
        for step in range(1, chips):
            peer_copy(c, step).wait_recv()
            total = total + from_peers[c, step - 1].astype(F32)
        average = total / workers
        moved = outer_beta * mom[:, :, cols(c)] + average
        nm[:, :, cols(c)] = moved
        part = anchor[:, r, :, cols(c)].astype(F32)
        na[:, r, :, cols(c)] = (
            part - outer_rate * (average + outer_beta * moved)
        ).astype(BF16)
        for step in range(1, chips):
            spread(c, r, step).start()
        across(c, r, 0).start()

    def pass_on(c):
        for step in range(1, chips):
            block = source(step) * 2 + core
            spread(c, block, step).wait_recv()
            across(c, block, step).start()

    def finish(c):
        for step in range(chips):
            across(c, source(step) * 2 + 1 - core, step).wait_recv()

    def backward(h):
        hc = pl.ds(h * DH, DH)
        kh = k[:, hc]
        vh = v[:, hc]
        ga = dot(g[...].reshape(length, width), w[h], 1, 1).astype(BF16)
        for t in range(length // tile):
            tr = pl.ds(t * tile, tile)
            gt = ga[t * tile:(t + 1) * tile]
            row = jnp.sum(gt.astype(F32) * att[tr, hc].astype(F32), axis=-1, keepdims=True)
            gp = dot(gt, vh, 1, 1)
            s = (probs[h, tr, :].astype(F32) * (gp - row)).astype(BF16)
            ds[tr, :] = s
            dq[tr, hc] = (dot(s, kh, 1, 0) * scale).astype(BF16)
        dv[:, hc] = dot(ga, probs[h], 0, 0).T.astype(BF16)
        dk[:, hc] = (dot(q[:, hc], ds[...], 0, 0) * scale).T.astype(BF16)

    ahead = min(2, CHUNKS)
    for c in range(ahead):
        own_send(c)
    for load in loads[:3]:
        load.wait()
    for h in range(heads):
        forward(h)
        if h < tensors - 1:
            relay(0, h)
    for s in range(heads, tensors - 1):
        relay(0, s)
    for load in loads[3:]:
        load.wait()
    stages = (pass_on, outer, pair_sum)

    def sync(slot, which):
        c = slot - (3 - which)
        if 0 <= c < CHUNKS:
            stages[which](c)

    for c in range(CHUNKS):
        if c > 0:
            for s in range(tensors - 1):
                relay(c, s)
        if c + ahead < CHUNKS:
            own_send(c + ahead)
        for which in range(3):
            sync(c, which)
        adam(c)
        partner_copy(c).start()
    for h in range(heads):
        backward(h)
        for which in range(3):
            sync(CHUNKS + h, which)
    for slot in range(CHUNKS + heads, CHUNKS + 3):
        for which in range(3):
            sync(slot, which)
    for c in range(CHUNKS):
        finish(c)
    drain_gather()
    for c in range(CHUNKS):
        partner_copy(c).wait_send()
        for step in range(1, chips):
            peer_copy(c, step).wait_send()
            spread(c, r, step).wait_send()
        for step in range(chips):
            across(c, source(step) * 2 + core, step).wait_send()

def store(*refs):
    n = (len(refs) - 1) // 2
    copies = [pltpu.make_async_copy(refs[j], refs[n + j], refs[-1].at[j]) for j in range(n)]
    for copy in copies:
        copy.start()
    for copy in copies:
        copy.wait()


def local(tensors, workers, queries, key_rows, value_rows, out_grads, inner_weights, adam_first,
          adam_second, anchor, momentum):
    length, inner = queries.shape[1:]
    rows, width = out_grads.shape[1:]
    heads = inner_weights.shape[1]
    slab = momentum.shape[1]
    chips = workers // 2
    cw = width // CHUNKS
    qs = (length, inner)
    ws = (heads, DH, width)
    an = (heads, workers, slab, width)
    ms = (heads, slab, width)
    S = jax.ShapeDtypeStruct
    hbm = pl.BlockSpec(memory_space=pltpu.HBM)
    V = pltpu.VMEM
    D = pltpu.SemaphoreType.DMA
    results = [(qs, BF16)] * 3 + [(ws, BF16)] * 2 + [(an, BF16), (ms, F32)]
    held = sum(math.prod(shape) * jnp.dtype(dtype).itemsize for shape, dtype in results)
    room = VMEM_BYTES - held - SPARE
    outs = pl.pallas_call(
        functools.partial(kernel, tensors, workers),
        out_shape=[V(shape, dtype) for shape, dtype in results],
        in_specs=[hbm] * 9,
        out_specs=[pl.BlockSpec(memory_space=V)] * 7,
        scratch_shapes=[
            V(qs, BF16), V(qs, BF16), V(qs, BF16), V((tensors, rows, width), BF16),
            V(ws, BF16), V(ws, BF16), V(ws, BF16), V(an, BF16), V(ms, F32),
            V((heads, length, length), BF16), V(qs, BF16), V((heads, DH, length), BF16),
            V((length, length), BF16),
            V((CHUNKS, 2, chips, heads, slab, cw), BF16),
            V((CHUNKS, chips, heads, slab, cw), BF16),
            V((CHUNKS, chips, heads, slab, cw), BF16),
            V((CHUNKS, chips - 1, heads, slab, cw), BF16),
            D((9,)),
            D((2, tensors - 1, CHUNKS)), D((2, tensors - 1, CHUNKS)),
            D((CHUNKS,)), D((CHUNKS,)),
            D((CHUNKS, chips - 1)), D((CHUNKS, chips - 1)),
            D((CHUNKS, chips - 1)), D((CHUNKS, chips - 1)),
            D((CHUNKS, chips)), D((CHUNKS, chips)),
        ],
        compiler_params=pltpu.CompilerParams(collective_id=0, has_side_effects=True, vmem_limit_bytes=room),
        name="sync",
    )(
        queries[0], key_rows[0], value_rows[0], out_grads[0], inner_weights[0], adam_first[0],
        adam_second[0], anchor.reshape(an), momentum,
    )
    dq, dk, dv, n1, n2, na, nm = pl.pallas_call(
        store,
        out_shape=[S(shape, dtype) for shape, dtype in results],
        in_specs=[pl.BlockSpec(memory_space=V)] * 7,
        out_specs=[hbm] * 7,
        scratch_shapes=[D((7,))],
        compiler_params=pltpu.CompilerParams(vmem_limit_bytes=2**20),
        name="store",
    )(*outs)
    return dq[None], dk[None], dv[None], n1[None], n2[None], na.reshape(anchor.shape), nm


def solution(mesh):
    workers = P("replica", "tensor", None, None)
    heads = P("replica", None, "tensor")
    specs = (
        heads, heads, heads, P("replica", "tensor", None), workers, workers, workers,
        P("tensor", None, None), P("tensor", "replica", None),
    )
    outs = (
        heads, heads, heads, workers, workers, P("tensor", None, None), P("tensor", "replica", None)
    )
    body = functools.partial(local, mesh.shape["tensor"], mesh.shape["replica"])
    return jax.shard_map(body, mesh=mesh, in_specs=specs, out_specs=outs, check_vma=False)
```

```python
import functools
import math

import jax
import jax.numpy as jnp
from jax import lax
from jax.experimental import pallas as pl
from jax.experimental.pallas import tpu as pltpu
from jax.sharding import PartitionSpec as P

DH = 128
CHUNKS = 2
TILE = 512
VMEM_BYTES = 67043328
SPARE = 2**17
MESH = pl.DeviceIdType.MESH

beta_first = 0.9
beta_second = 0.95
correct_first = 0.9999734386011124
correct_second = 0.994079470779666
inner_rate = 0.01
decay_rate = 0.1
epsilon = 1e-08
outer_rate = 0.7
outer_beta = 0.9

F32 = jnp.float32
BF16 = jnp.bfloat16


def dot(a, b, ca, cb):
    return lax.dot_general(a, b, (((ca,), (cb,)), ((), ())), preferred_element_type=F32)


def kernel(
    tensors,
    workers,
    q_hbm, k_hbm, v_hbm, g_hbm, w_hbm, m1_hbm, m2_hbm, anchor_hbm, mom_hbm,
    dq, dk, dv, n1, n2, na, nm,
    q, k, v, g, w, m1, m2, anchor, mom,
    probs, att, att_t, ds, delta, from_partner, pair, from_peers,
    in_sem,
    g_send, g_recv, p_send, p_recv, r_send, r_recv, a_send, a_recv, f_send, f_recv,
):
    heads = w.shape[0]
    width = g.shape[2]
    length = q.shape[0]
    rows = g.shape[1]
    slab = mom.shape[1]
    chips = workers // 2
    cw = width // CHUNKS
    scale = 1.0 / math.sqrt(DH)

    i = lax.axis_index("tensor")
    r = lax.axis_index("replica")
    chip = r // 2
    core = r % 2
    partner = chip * 2 + 1 - core
    has_left = i > 0
    has_right = i < tensors - 1

    def peer(step):
        return lax.rem(chip + step, chips) * 2 + core

    def source(step):
        return lax.rem(chip + chips - step, chips)

    barrier = pltpu.get_barrier_semaphore()

    @pl.when(has_left)
    def _():
        pl.semaphore_signal(barrier, inc=1, device_id={"tensor": i - 1}, device_id_type=MESH)

    @pl.when(has_right)
    def _():
        pl.semaphore_signal(barrier, inc=1, device_id={"tensor": i + 1}, device_id_type=MESH)

    pl.semaphore_signal(barrier, inc=1, device_id={"replica": partner}, device_id_type=MESH)
    for step in range(1, chips):
        pl.semaphore_signal(barrier, inc=1, device_id={"replica": peer(step)}, device_id_type=MESH)

    loads = [
        pltpu.make_async_copy(s, d, in_sem.at[n])
        for n, (s, d) in enumerate(
            [
                (q_hbm, q), (k_hbm, k), (v_hbm, v), (g_hbm, g.at[i]), (w_hbm, w),
                (m1_hbm, m1), (m2_hbm, m2), (anchor_hbm, anchor), (mom_hbm, mom),
            ]
        )
    ]
    for load in loads:
        load.start()

    inner = jnp.logical_and(has_left, has_right)

    @pl.when(inner)
    def _():
        pl.semaphore_wait(barrier, chips + 2)

    @pl.when(jnp.logical_not(inner))
    def _():
        pl.semaphore_wait(barrier, chips + 1)

    def cols(c):
        return pl.ds(c * cw, cw)

    def right_copy(block, s, c, own=False):
        src = g_hbm.at[:, cols(c)] if own else g.at[block, :, cols(c)]
        return pltpu.make_async_remote_copy(
            src_ref=src, dst_ref=g.at[block, :, cols(c)],
            send_sem=g_send.at[0, s, c], recv_sem=g_recv.at[0, s, c],
            device_id={"tensor": i + 1}, device_id_type=MESH,
        )

    def left_copy(block, s, c, own=False):
        src = g_hbm.at[:, cols(c)] if own else g.at[block, :, cols(c)]
        return pltpu.make_async_remote_copy(
            src_ref=src, dst_ref=g.at[block, :, cols(c)],
            send_sem=g_send.at[1, s, c], recv_sem=g_recv.at[1, s, c],
            device_id={"tensor": i - 1}, device_id_type=MESH,
        )

    def own_send(c):
        @pl.when(has_right)
        def _():
            right_copy(i, 0, c, True).start()

        @pl.when(has_left)
        def _():
            left_copy(i, 0, c, True).start()

    def relay(c, s):
        @pl.when(i - 1 - s >= 0)
        def _():
            block = i - 1 - s
            right_copy(block, s, c).wait_recv()
            if s + 1 <= tensors - 2:
                @pl.when(has_right)
                def _():
                    right_copy(block, s + 1, c).start()

        @pl.when(i + 1 + s < tensors)
        def _():
            block = i + 1 + s
            left_copy(block, s, c).wait_recv()
            if s + 1 <= tensors - 2:
                @pl.when(has_left)
                def _():
                    left_copy(block, s + 1, c).start()

    def drain_gather():
        for c in range(CHUNKS):
            for s in range(tensors - 1):
                @pl.when(jnp.logical_and(has_right, i - s >= 0))
                def _():
                    right_copy(i - s, s, c, s == 0).wait_send()

                @pl.when(jnp.logical_and(has_left, i + s < tensors))
                def _():
                    left_copy(i + s, s, c, s == 0).wait_send()

    tile = TILE

    def forward(h):
        hc = pl.ds(h * DH, DH)
        kh = k[:, hc]
        vh = v[:, hc]
        for t in range(length // tile):
            tr = pl.ds(t * tile, tile)
            s = dot(q[tr, hc], kh, 1, 1) * scale
            e = jnp.exp(s - jnp.max(s, axis=-1, keepdims=True))
            p = (e / jnp.sum(e, axis=-1, keepdims=True)).astype(BF16)
            probs[h, tr, :] = p
            a = dot(p, vh, 1, 0)
            att[tr, hc] = a.astype(BF16)
            att_t[h, :, tr] = a.T.astype(BF16)

    def adam(c):
        def body(h, carry):
            gb = g[:, :, cols(c)].reshape(length, cw)
            grad = dot(att_t[h], gb, 1, 0)
            first = beta_first * m1[h, :, cols(c)].astype(F32) + (1.0 - beta_first) * grad
            second = (
                beta_second * m2[h, :, cols(c)].astype(F32) + (1.0 - beta_second) * grad * grad
            )
            n1[h, :, cols(c)] = first.astype(BF16)
            n2[h, :, cols(c)] = second.astype(BF16)
            old = w[h, :, cols(c)].astype(F32)
            stepped = old - inner_rate * (
                first / correct_first / (jnp.sqrt(second / correct_second) + epsilon)
                + decay_rate * old
            )
            an = anchor[h, :, :, cols(c)].astype(F32)
            d = an - stepped.reshape(workers, slab, cw)
            for x in range(workers):
                delta[c, x % 2, x // 2, h] = d[x].astype(BF16)
            return carry

        lax.fori_loop(0, heads, body, 0)

    def partner_copy(c):
        return pltpu.make_async_remote_copy(
            src_ref=delta.at[c, 1 - core], dst_ref=from_partner.at[c],
            send_sem=p_send.at[c], recv_sem=p_recv.at[c],
            device_id={"replica": partner}, device_id_type=MESH,
        )

    def peer_copy(c, step):
        return pltpu.make_async_remote_copy(
            src_ref=pair.at[c, lax.rem(chip + step, chips)], dst_ref=from_peers.at[c, step - 1],
            send_sem=r_send.at[c, step - 1], recv_sem=r_recv.at[c, step - 1],
            device_id={"replica": peer(step)}, device_id_type=MESH,
        )

    def pair_sum(c):
        partner_copy(c).wait_recv()
        for x in range(chips):
            pair[c, x] = (
                delta[c, core, x].astype(F32) + from_partner[c, x].astype(F32)
            ).astype(BF16)
        for step in range(1, chips):
            peer_copy(c, step).start()

    def spread(c, block, step):
        return pltpu.make_async_remote_copy(
            src_ref=na.at[:, block, :, cols(c)], dst_ref=na.at[:, block, :, cols(c)],
            send_sem=a_send.at[c, step - 1], recv_sem=a_recv.at[c, step - 1],
            device_id={"replica": peer(step)}, device_id_type=MESH,
        )

    def across(c, block, step):
        return pltpu.make_async_remote_copy(
            src_ref=na.at[:, block, :, cols(c)], dst_ref=na.at[:, block, :, cols(c)],
            send_sem=f_send.at[c, step], recv_sem=f_recv.at[c, step],
            device_id={"replica": partner}, device_id_type=MESH,
        )

    def outer(c):
        total = delta[c, core, chip].astype(F32) + from_partner[c, chip].astype(F32)
        for step in range(1, chips):
            peer_copy(c, step).wait_recv()
            total = total + from_peers[c, step - 1].astype(F32)
        average = total / workers
        moved = outer_beta * mom[:, :, cols(c)] + average
        nm[:, :, cols(c)] = moved
        part = anchor[:, r, :, cols(c)].astype(F32)
        na[:, r, :, cols(c)] = (
            part - outer_rate * (average + outer_beta * moved)
        ).astype(BF16)
        for step in range(1, chips):
            spread(c, r, step).start()
        across(c, r, 0).start()

    def pass_on(c):
        for step in range(1, chips):
            block = source(step) * 2 + core
            spread(c, block, step).wait_recv()
            across(c, block, step).start()

    def finish(c):
        for step in range(chips):
            across(c, source(step) * 2 + 1 - core, step).wait_recv()

    def backward(h):
        hc = pl.ds(h * DH, DH)
        kh = k[:, hc]
        vh = v[:, hc]
        ga = dot(g[...].reshape(length, width), w[h], 1, 1).astype(BF16)
        for t in range(length // tile):
            tr = pl.ds(t * tile, tile)
            gt = ga[t * tile:(t + 1) * tile]
            row = jnp.sum(gt.astype(F32) * att[tr, hc].astype(F32), axis=-1, keepdims=True)
            gp = dot(gt, vh, 1, 1)
            s = (probs[h, tr, :].astype(F32) * (gp - row)).astype(BF16)
            ds[tr, :] = s
            dq[tr, hc] = (dot(s, kh, 1, 0) * scale).astype(BF16)
        dv[:, hc] = dot(ga, probs[h], 0, 0).T.astype(BF16)
        dk[:, hc] = (dot(q[:, hc], ds[...], 0, 0) * scale).T.astype(BF16)

    ahead = min(2, CHUNKS)
    for c in range(ahead):
        own_send(c)
    for load in loads[:3]:
        load.wait()
    for h in range(heads):
        forward(h)
        if h < tensors - 1:
            relay(0, h)
    for s in range(heads, tensors - 1):
        relay(0, s)
    for load in loads[3:]:
        load.wait()
    for c in range(CHUNKS):
        if c > 0:
            for s in range(tensors - 1):
                if s == tensors - 2:
                    pair_sum(c - 1)
                relay(c, s)
        if c + ahead < CHUNKS:
            own_send(c + ahead)
        adam(c)
        partner_copy(c).start()
        if c > 0:
            outer(c - 1)
        if 0 < c < CHUNKS - 1:
            pass_on(c - 1)
    last = CHUNKS - 1
    for h in range(heads):
        backward(h)
        if h == 0:
            pair_sum(last)
        if h == min(1, heads - 1):
            if CHUNKS > 1:
                pass_on(last - 1)
            outer(last)
        if h == min(3, heads - 1):
            pass_on(last)
    for c in range(CHUNKS):
        finish(c)
    drain_gather()
    for c in range(CHUNKS):
        partner_copy(c).wait_send()
        for step in range(1, chips):
            peer_copy(c, step).wait_send()
            spread(c, r, step).wait_send()
        for step in range(chips):
            across(c, source(step) * 2 + core, step).wait_send()

def store(*refs):
    n = (len(refs) - 1) // 2
    copies = [pltpu.make_async_copy(refs[j], refs[n + j], refs[-1].at[j]) for j in range(n)]
    for copy in copies:
        copy.start()
    for copy in copies:
        copy.wait()


def local(tensors, workers, queries, key_rows, value_rows, out_grads, inner_weights, adam_first,
          adam_second, anchor, momentum):
    length, inner = queries.shape[1:]
    rows, width = out_grads.shape[1:]
    heads = inner_weights.shape[1]
    slab = momentum.shape[1]
    chips = workers // 2
    cw = width // CHUNKS
    qs = (length, inner)
    ws = (heads, DH, width)
    an = (heads, workers, slab, width)
    ms = (heads, slab, width)
    S = jax.ShapeDtypeStruct
    hbm = pl.BlockSpec(memory_space=pltpu.HBM)
    V = pltpu.VMEM
    D = pltpu.SemaphoreType.DMA
    results = [(qs, BF16)] * 3 + [(ws, BF16)] * 2 + [(an, BF16), (ms, F32)]
    held = sum(math.prod(shape) * jnp.dtype(dtype).itemsize for shape, dtype in results)
    room = VMEM_BYTES - held - SPARE
    outs = pl.pallas_call(
        functools.partial(kernel, tensors, workers),
        out_shape=[V(shape, dtype) for shape, dtype in results],
        in_specs=[hbm] * 9,
        out_specs=[pl.BlockSpec(memory_space=V)] * 7,
        scratch_shapes=[
            V(qs, BF16), V(qs, BF16), V(qs, BF16), V((tensors, rows, width), BF16),
            V(ws, BF16), V(ws, BF16), V(ws, BF16), V(an, BF16), V(ms, F32),
            V((heads, length, length), BF16), V(qs, BF16), V((heads, DH, length), BF16),
            V((length, length), BF16),
            V((CHUNKS, 2, chips, heads, slab, cw), BF16),
            V((CHUNKS, chips, heads, slab, cw), BF16),
            V((CHUNKS, chips, heads, slab, cw), BF16),
            V((CHUNKS, chips - 1, heads, slab, cw), BF16),
            D((9,)),
            D((2, tensors - 1, CHUNKS)), D((2, tensors - 1, CHUNKS)),
            D((CHUNKS,)), D((CHUNKS,)),
            D((CHUNKS, chips - 1)), D((CHUNKS, chips - 1)),
            D((CHUNKS, chips - 1)), D((CHUNKS, chips - 1)),
            D((CHUNKS, chips)), D((CHUNKS, chips)),
        ],
        compiler_params=pltpu.CompilerParams(collective_id=0, has_side_effects=True, vmem_limit_bytes=room),
        name="sync",
    )(
        queries[0], key_rows[0], value_rows[0], out_grads[0], inner_weights[0], adam_first[0],
        adam_second[0], anchor.reshape(an), momentum,
    )
    dq, dk, dv, n1, n2, na, nm = pl.pallas_call(
        store,
        out_shape=[S(shape, dtype) for shape, dtype in results],
        in_specs=[pl.BlockSpec(memory_space=V)] * 7,
        out_specs=[hbm] * 7,
        scratch_shapes=[D((7,))],
        compiler_params=pltpu.CompilerParams(vmem_limit_bytes=2**20),
        name="store",
    )(*outs)
    return dq[None], dk[None], dv[None], n1[None], n2[None], na.reshape(anchor.shape), nm


def solution(mesh):
    workers = P("replica", "tensor", None, None)
    heads = P("replica", None, "tensor")
    specs = (
        heads, heads, heads, P("replica", "tensor", None), workers, workers, workers,
        P("tensor", None, None), P("tensor", "replica", None),
    )
    outs = (
        heads, heads, heads, workers, workers, P("tensor", None, None), P("tensor", "replica", None)
    )
    body = functools.partial(local, mesh.shape["tensor"], mesh.shape["replica"])
    return jax.shard_map(body, mesh=mesh, in_specs=specs, out_specs=outs, check_vma=False)
```
